32 devices in a mesh: row: 8 (over z, x), col: 4 (over y, core).
Axes of the slice: x: 2, y: 2, z: 4, core: 2. Of those that a mesh axis runs over, the one named last changes fastest.
Arguments:
- matrix: float32 [8192, 4096], P('row', 'col'), may hold values from -6 to 6
- tile_mask: int32 [64, 32], P('row', 'col'), may hold values 0 or 1
- panel_order: int32 [32], replicated, may hold values from 0 to 31, each once
Outputs:
- factors: float32 [4, 128, 128], replicated
- projections: float32 [4, 128, 4096], P(None, None, 'col')
- remainder: float32 [8192, 4096], P('row', 'col')
The draws below stay inside these ranges and needn't reach their ends.
Inputs may be any that keep to these rules, and one draw needn't show every extreme that they name: panel_order is a permutation of the column blocks, so the 4 panels differ, and every column block among the first 4 of panel_order has at least one nonzero tile in tile_mask.
All inputs are finite; a program needn't handle non-finite values. No bound on the sum of `tile_mask` on one device may be relied on, other than what follows from the above.
Results may differ from the reference program's by a relative error of at most 0.0001.
Values sent between devices are 32-bit elements; how exact they have to be, the bound alone decides.
No kernel may reach another device: no remote copies, remote signals or barrier semaphores. Data moves between devices by JAX's collectives and lax.ppermute only.
A program may use at most 64 MiB of HBM per device.

```python
import jax
import jax.numpy as jnp
from jax import lax

PANELS = 4
ROWS = 8192
NB = 32
NCOL = 4096
ROW_TILES = 64


def set_ends(values, key, low, largest):
    longest = values.shape.index(max(values.shape))
    spots = []
    for shift in (0, 1):
        where = [jax.random.randint(jax.random.fold_in(key, axis), (), 0, length) for axis, length in enumerate(values.shape)]
        where[longest] = (where[longest] + shift) % values.shape[longest]
        spots.append(tuple(where))
    return values.at[spots[0]].set(low).at[spots[1]].set(largest)


def shard_levels(stream_key, dims, shards, least, high):
    factor_of = 1.0
    for position, blocks in shards:
        heights = jax.random.uniform(jax.random.fold_in(jax.random.fold_in(stream_key, 6), position), (blocks,), jnp.float32, least / len(shards), high / len(shards))
        factor_of = factor_of * jnp.repeat(jnp.exp(heights), dims[position] // blocks).reshape((-1,) + (1,) * (len(dims) - 1 - position))
    return factor_of


def scatter_about(key, dims, deviation, bound, cuts=(), held_as=jnp.bfloat16):
    factor_of = shard_levels(key, dims, cuts, -0.22, 0.18) if cuts else 1.0
    array = jax.random.normal(key, dims, jnp.float32) * deviation * factor_of
    return jnp.minimum(jnp.maximum(array, -bound), bound).astype(held_as)


def setup_inputs(seed: int = 0) -> dict:
    key_list = jax.random.split(jax.random.key(seed), 4)
    matrix = scatter_about(key_list[0], (ROWS, NCOL), 1.0, 6.0, ((0, 8), (1, 4)), jnp.float32)
    tile_mask = set_ends((jax.random.randint(key_list[1], (ROW_TILES, NB), 0, 4) < 3).astype(jnp.int32), jax.random.fold_in(key_list[1], 1), 0, 1)
    panel_order = jax.random.permutation(key_list[2], NB).astype(jnp.int32)
    return {"matrix": matrix, "tile_mask": tile_mask, "panel_order": panel_order}


def reference(matrix, tile_mask, panel_order):
    hi = lax.Precision.HIGHEST
    row_tiles, nblocks = tile_mask.shape
    tile = matrix.shape[1] // nblocks
    system = (matrix.reshape(row_tiles, tile, nblocks, tile) * tile_mask.astype(jnp.float32)[:, None, :, None]).reshape(matrix.shape)
    factor_list = []
    proj_list = []
    for p in range(PANELS):
        start = (panel_order[p] * tile).astype(jnp.int32)
        panel = lax.dynamic_slice_in_dim(system, start, tile, 1)
        gram = jnp.dot(panel.T, panel, precision=hi)
        lower = jnp.linalg.cholesky(gram)
        basis_t = jax.scipy.linalg.solve_triangular(lower, panel.T, lower=True)
        proj = jnp.dot(basis_t, system, precision=hi)
        system = system - jnp.dot(basis_t.T, proj, precision=hi)
        factor_list.append(lower.T)
        proj_list.append(proj)
    return (jnp.stack(factor_list), jnp.stack(proj_list), system)
```

```python
import jax
import jax.numpy as jnp
from jax import lax
from jax.sharding import PartitionSpec as P

PANELS = 4
HI = lax.Precision.HIGHEST
MID = lax.Precision.HIGH


def swap(x, axis, bit):
    size = lax.axis_size(axis)
    return lax.ppermute(x, axis, [(i, i ^ bit) for i in range(size)])


def bits_of(size):
    return [1 << k for k in range(size.bit_length() - 1)]


def has(axis, bit):
    return (lax.axis_index(axis) // bit) % 2


def gather_panels(mine):
    size = lax.axis_size("col")
    pair, *others = bits_of(size)
    both = mine + swap(mine, "col", pair)
    half = both.shape[1] // 2
    core = has("col", pair)
    part = lax.dynamic_slice_in_dim(both, core * half, half, 1)
    for bit in others:
        part = part + swap(part, "col", bit)
    other = swap(part, "col", pair)
    return jnp.where(core == 0, jnp.concatenate([part, other], 1), jnp.concatenate([other, part], 1))


def sum_rows(parts, orders):
    parts = list(parts)
    steps = len(orders[0])
    for s in range(steps):
        for n, order in enumerate(orders):
            bit = order[s]
            half = parts[n].shape[0] // 2
            b = has("row", bit)
            send = lax.dynamic_slice_in_dim(parts[n], (1 - b) * half, half, 0)
            keep = lax.dynamic_slice_in_dim(parts[n], b * half, half, 0)
            parts[n] = keep + swap(send, "row", bit)
    for s in reversed(range(steps)):
        for n, order in enumerate(orders):
            bit = order[s]
            b = has("row", bit)
            mine, other = parts[n], swap(parts[n], "row", bit)
            parts[n] = jnp.where(b == 0, jnp.concatenate([mine, other], 0), jnp.concatenate([other, mine], 0))
    return parts


def factor(gram, tile):
    size = gram.shape[0]
    n = size // tile
    rows = jnp.concatenate([gram, jnp.eye(size, dtype=gram.dtype)], 1)
    eye = jnp.eye(tile, dtype=gram.dtype)
    factor_list = []
    inverse_list = []
    for p in range(n):
        lower = jnp.linalg.cholesky(rows[:tile, p * tile : (p + 1) * tile])
        inv = jax.scipy.linalg.solve_triangular(lower, eye, lower=True)
        factor_list.append(lower.T)
        top = jnp.dot(inv, rows[:tile], precision=HI)
        inverse_list.append(top[:, size:])
        if p + 1 < n:
            rest = top[:, (p + 1) * tile : size]
            rows = rows[tile:] - lax.dot_general(rest, top, (((0,), (0,)), ((), ())), precision=HI)
    return jnp.stack(factor_list), jnp.concatenate(inverse_list, 0)


def on_device(matrix, tile_mask, panel_order):
    rows, cols = matrix.shape
    nb_local = tile_mask.shape[1]
    tile = cols // nb_local
    work = (
        matrix.reshape(rows // tile, tile, nb_local, tile)
        * tile_mask.astype(jnp.float32)[:, None, :, None]
    ).reshape(rows, cols)
    me = lax.axis_index("col")
    mine = []
    for p in range(PANELS):
        b = panel_order[p]
        cut = lax.dynamic_slice_in_dim(work, b % nb_local * tile, tile, 1)
        mine.append(jnp.where(b // nb_local == me, cut, jnp.zeros_like(cut)))
    panels = gather_panels(jnp.concatenate(mine, 1))
    width = PANELS * tile
    order = bits_of(lax.axis_size("row"))
    share = width // lax.axis_size("col")
    part = lax.dynamic_slice_in_dim(panels, me * share, share, 1)
    gram = lax.dot_general(part, panels, (((0,), (0,)), ((), ())), precision=HI)
    (gram,) = sum_rows([gram], [order])
    for bit in bits_of(lax.axis_size("col")):
        b = has("col", bit)
        other = swap(gram, "col", bit)
        gram = jnp.where(b == 0, jnp.concatenate([gram, other], 0), jnp.concatenate([other, gram], 0))
    half = width // 2
    cross = lax.dot_general(panels, work, (((0,), (0,)), ((), ())), precision=MID)
    cross = sum_rows([cross[:half], cross[half:]], [order, [order[1], order[0]] + order[2:]])
    cross = jnp.concatenate(cross, 0)
    factors, inverse = factor(gram, tile)
    basis = lax.dot_general(panels, inverse, (((1,), (1,)), ((), ())), precision=MID)
    proj = jnp.dot(inverse, cross, precision=MID)
    work = work - jnp.dot(basis, proj, precision=MID)
    return factors, proj.reshape(PANELS, tile, cols), work


def solution(mesh):
    return jax.shard_map(
        on_device,
        mesh=mesh,
        in_specs=(P("row", "col"), P("row", "col"), P()),
        out_specs=(P(), P(None, None, "col"), P("row", "col")),
        check_vma=False,
    )
```

```python
import jax
import jax.numpy as jnp
from jax import lax
from jax.experimental import pallas as pl
from jax.experimental.pallas import tpu as pltpu
from jax.sharding import PartitionSpec as P

PANELS = 4
SUB = 8
HI = lax.Precision.HIGHEST
MID = lax.Precision.HIGH


def swap(x, axis, bit, name="swap"):
    size = lax.axis_size(axis)
    with jax.named_scope(name):
        return lax.ppermute(x, axis, [(i, i ^ bit) for i in range(size)])


def bits_of(size):
    return [1 << k for k in range(size.bit_length() - 1)]


def has(axis, bit):
    return (lax.axis_index(axis) // bit) % 2


def after(x, *others):
    return lax.optimization_barrier((x, *others))[0]


def halves(x, b):
    half = x.shape[0] // 2
    return lax.dynamic_slice_in_dim(x, b * half, half, 0), lax.dynamic_slice_in_dim(x, (1 - b) * half, half, 0)


def join(mine, other, b):
    return jnp.where(b == 0, jnp.concatenate([mine, other], 0), jnp.concatenate([other, mine], 0))


def cut_kernel(order_ref, mask_ref, matrix_ref, out_ref, *, first):
    rows, tile = out_ref.shape
    nb = mask_ref.shape[1]
    b = order_ref[first + pl.program_id(0)]
    mine = jnp.where(b // nb == lax.axis_index("col"), 1.0, 0.0)
    for t in range(rows // tile):
        keep = mine * mask_ref[t, b % nb].astype(jnp.float32)
        s = slice(t * tile, (t + 1) * tile)
        out_ref[s, :] = matrix_ref[s, :] * keep


def cut_panels(matrix, tile_mask, panel_order, first, count):
    rows, cols = matrix.shape
    nb = tile_mask.shape[1]
    tile = cols // nb
    return pl.pallas_call(
        lambda *refs: cut_kernel(*refs, first=first),
        grid_spec=pltpu.PrefetchScalarGridSpec(
            num_scalar_prefetch=2,
            grid=(count,),
            in_specs=[pl.BlockSpec((rows, tile), lambda p, order, mask: (0, order[first + p] % nb))],
            out_specs=pl.BlockSpec((rows, tile), lambda p, order, mask: (0, p)),
        ),
        out_shape=jax.ShapeDtypeStruct((rows, count * tile), matrix.dtype),
        name=f"cut{first}",
    )(panel_order, tile_mask, matrix)


def eliminate(a_ref, i_ref, u_ref, v_ref):
    tile = a_ref.shape[0]
    shape = (SUB, tile)
    sub = lax.broadcasted_iota(jnp.int32, shape, 0)
    for r0 in range(0, tile, SUB):
        a8, i8 = a_ref[r0 : r0 + SUB, :], i_ref[r0 : r0 + SUB, :]
        c = {}
        for j in range(SUB):
            col = jnp.broadcast_to(a8[:, r0 + j : r0 + j + 1], shape)
            for i in range(j, SUB):
                c[i, j] = jnp.broadcast_to(col[i : i + 1, :], shape)
        y = [[jnp.broadcast_to(x[k : k + 1, :], shape) for x in (a8, i8)] for k in range(SUB)]
        inv, mult = {}, {}
        for k in range(SUB):
            inv[k] = 1.0 / c[k, k]
            for j in range(k + 1, SUB):
                mult[j, k] = c[j, k] * inv[k]
            for j in range(k + 1, SUB):
                for i in range(j, SUB):
                    c[i, j] = c[i, j] - mult[i, k] * c[j, k]
                y[j] = [s - mult[j, k] * t for s, t in zip(y[j], y[k])]
        v = [None] * SUB
        for j in reversed(range(SUB)):
            v[j] = [inv[j] * s for s in y[j]]
            for k in reversed(range(j + 1, SUB)):
                v[j] = [s - mult[k, j] * t for s, t in zip(v[j], v[k])]
        for h, out in enumerate((u_ref, v_ref)):
            rows = None
            for k in range(SUB):
                x = y[k][h] * lax.rsqrt(c[k, k])
                rows = x if rows is None else jnp.where(sub == k, x, rows)
            out[r0 : r0 + SUB, :] = rows
        for t0 in range(r0 + SUB, tile, SUB):
            a, i = a_ref[t0 : t0 + SUB, :], i_ref[t0 : t0 + SUB, :]
            left = a
            for j in range(SUB):
                w = jnp.broadcast_to(left[:, r0 + j : r0 + j + 1], shape)
                a = a - w * v[j][0]
                i = i - w * v[j][1]
            a_ref[t0 : t0 + SUB, :] = a
            i_ref[t0 : t0 + SUB, :] = i

def dot_t(a, b, precision=HI):
    return lax.dot_general(a, b, (((0,), (0,)), ((), ())), precision=precision)


def dot_nt(a, b, precision=HI):
    return lax.dot_general(a, b, (((1,), (1,)), ((), ())), precision=precision)


def factor_kernel(*refs, panel, tile):
    n_in = (2, 2, 4, 4)[panel]
    n_out = (4, 2, 4, 2)[panel]
    ins, outs, (a_ref, i_ref, u_ref, v_ref, *left) = refs[:n_in], refs[n_in : n_in + n_out], refs[n_in + n_out :]
    row = lax.broadcasted_iota(jnp.int32, (tile, tile), 0)
    col = lax.broadcasted_iota(jnp.int32, (tile, tile), 1)
    if panel % 2 == 0:
        (gram_ref,) = left
        core = lax.axis_index("col") % 2
        half = ins[0].shape[0]
        gram_ref[pl.ds(pl.multiple_of(core * half, half), half), :] = ins[0][...]
        gram_ref[pl.ds(pl.multiple_of((1 - core) * half, half), half), :] = ins[1][...]
    if panel == 0:
        rest, old = gram_ref[...], None
    elif panel == 1:
        rest, old = ins[0][...], ins[1][...]
    elif panel == 2:
        upper, lower = ins[2][...], ins[3][...]
        side = gram_ref[:, : 2 * tile]
        across = jnp.concatenate([dot_nt(upper, side[:, :tile]), dot_nt(lower, side)], 0)
        rest = gram_ref[:, 2 * tile :] - dot_t(across, across)
        old = -jnp.concatenate(
            [dot_t(across[:tile], upper) + dot_t(across[tile:], lower[:, :tile]), dot_t(across[tile:], lower[:, tile:])], 1
        )
    else:
        rest, old = ins[0][...], ins[1][...]
    a_ref[...] = rest[:tile, :tile]
    i_ref[...] = jnp.where(row == col, 1.0, 0.0)
    eliminate(a_ref, i_ref, u_ref, v_ref)
    outs[0][...] = jnp.where(col >= row, u_ref[...], 0.0)
    v = v_ref[...]
    top = v if old is None else jnp.concatenate([jnp.dot(v, old[:tile], precision=HI), v], 1)
    if panel == 3:
        outs[1][:tile, : 3 * tile] = ins[2][...]
        outs[1][:tile, 3 * tile :] = jnp.zeros((tile, tile), v.dtype)
        outs[1][tile:, :] = top
        return
    outs[1][...] = top
    if panel == 1:
        return
    across = jnp.dot(v, rest[:tile, tile:], precision=HI)
    outs[2][...] = rest[tile:, tile:] - dot_t(across, across)
    below = -dot_t(across, top)
    if old is not None:
        below = below + jnp.concatenate([old[tile:], jnp.zeros((tile, tile), v.dtype)], 1)
    outs[3][...] = below


def factor_step(panel, tile, dtype, *operands):
    f32 = lambda *shape: jax.ShapeDtypeStruct(shape, dtype)
    wide = (panel + 1) * tile
    out = {
        0: (f32(tile, tile), f32(tile, wide), f32(tile, tile), f32(tile, wide)),
        1: (f32(tile, tile), f32(tile, wide)),
        2: (f32(tile, tile), f32(tile, wide), f32(tile, tile), f32(tile, wide)),
        3: (f32(tile, tile), f32(2 * tile, wide)),
    }[panel]
    scratch = [pltpu.VMEM((tile, tile), dtype)] * 4
    if panel % 2 == 0:
        scratch.append(pltpu.VMEM((2 * tile, (panel + 2) * tile), dtype))
    return pl.pallas_call(
        lambda *refs: factor_kernel(*refs, panel=panel, tile=tile),
        out_shape=out,
        scratch_shapes=scratch,
        name=f"factor{panel}",
    )(*operands)


def on_device(matrix, tile_mask, panel_order):
    rows, cols = matrix.shape
    nb_local = tile_mask.shape[1]
    tile = cols // nb_local
    dtype = matrix.dtype
    order = bits_of(lax.axis_size("row"))
    pair, *others = bits_of(lax.axis_size("col"))
    core = has("col", pair)
    shares = lax.axis_size("col")
    index = core * (shares // 2) + lax.axis_index("col") // 2

    def share_of(gram):
        part = gram.shape[0] // shares
        return lax.dynamic_slice_in_dim(gram, index * part, part, 0)

    def side_by_side(mine, other):
        return jnp.where(core == 0, jnp.concatenate([mine, other], 1), jnp.concatenate([other, mine], 1))

    mine = [cut_panels(matrix, tile_mask, panel_order, h, 2) for h in range(0, PANELS, 2)]
    work = (
        matrix.reshape(rows // tile, tile, nb_local, tile)
        * tile_mask.astype(jnp.float32)[:, None, :, None]
    ).reshape(rows, cols)
    both = [mine[h] + swap(mine[h], "col", pair, f"core_in{h}") for h in range(2)]
    part = [lax.dynamic_slice_in_dim(x, core * tile, tile, 1) for x in both]
    for bit in others:
        part[0] = part[0] + swap(part[0], "col", bit, "chip0")
    first = side_by_side(part[0], swap(part[0], "col", pair, "core_out0"))

    last = len(order) - 1
    swapped = [order[1], order[0]] + order[2:]

    def halve(x, bit, name, *gates):
        keep, send = halves(x, has("row", bit))
        got = swap(send, "row", bit, name)
        return after(keep, *gates) + got

    def add(x, bit, name, *gates):
        got = swap(x, "row", bit, name)
        return after(x, *gates) + got

    def double(x, axis, bit, name, *gates):
        got = swap(x, axis, bit, name)
        return join(after(x, *gates), got, has(axis, bit))

    early = order[:last]
    sent_a, sent_b = [], []

    gram_a = share_of(dot_t(first, first))
    cross_a = dot_t(after(first, gram_a), work)
    wait = [(cross_a,)] + [()] * last
    for k, bit in enumerate(order):
        sent_a.append(gram_a)
        gram_a = add(gram_a, bit, f"gram_a{k}", *wait[k])
    part[1] = after(part[1], part[0])
    for k, bit in enumerate(others):
        got = swap(part[1], "col", bit, "chip1")
        part[1] = (part[1] if k else after(part[1], sent_a[last])) + got
    second = side_by_side(part[1], swap(part[1], "col", pair, "core_out1"))
    for bit in others:
        gram_a = double(gram_a, "col", bit, "gram_a_chip")
    gram_a_other = swap(gram_a, "col", pair, "gram_a_core")

    gram_b = jnp.concatenate([share_of(dot_t(second, first)), share_of(dot_t(second, second))], 1)
    cross_b = dot_t(after(second, gram_b), work)
    cross_a = halve(cross_a, early[0], "cross_a0", gram_b)
    f0, top0, rest, below = factor_step(0, tile, dtype, after(gram_a, cross_b), gram_a_other)
    gram_b = add(gram_b, order[0], "gram_b0", f0)
    for bit in early[1:]:
        cross_a = halve(cross_a, bit, "cross_a1", f0)
    f1, top1 = factor_step(1, tile, dtype, after(rest, gram_b, cross_a), below)
    for k, bit in enumerate(order[1:]):
        gram_b = add(gram_b, bit, f"gram_b{k + 1}", *((f1,) if k == 0 else ()))
        if k == 0:
            third = gram_b
    cross_b = halve(cross_b, early[0], "cross_b0", third)
    for bit in early[1:]:
        cross_b = halve(cross_b, bit, "cross_b1", gram_b)
    cross_a = add(cross_a, order[last], "cross_a_z", gram_b)
    for bit in others:
        gram_b = double(gram_b, "col", bit, "gram_b_chip")
    gram_b_other = swap(gram_b, "col", pair, "gram_b_core")
    f2, top2, rest, below = factor_step(2, tile, dtype, gram_b, gram_b_other, top0, top1)
    for k, bit in enumerate(reversed(early)):
        cross_a = double(cross_a, "row", bit, f"cross_a_back{k}", f2)
        if k == 0:
            back_a = cross_a
    cross_b = add(cross_b, order[last], "cross_b_z", f2)
    f3, lower = factor_step(3, tile, dtype, after(rest, back_a, cross_b), below, top2, top2)
    for k, bit in enumerate(reversed(early)):
        cross_b = double(cross_b, "row", bit, f"cross_b_back{k}", f3)
    upper = jnp.concatenate([jnp.concatenate([top0, jnp.zeros_like(top0)], 1), top1], 0)
    width = 2 * tile
    basis1 = dot_nt(first, upper)
    basis2 = dot_nt(first, lower[:, :width]) + dot_nt(second, lower[:, width:])
    proj1 = jnp.dot(upper, cross_a, precision=HI)
    work = lax.optimization_barrier(work - jnp.dot(basis1, proj1, precision=MID))
    proj2 = jnp.dot(lower[:, :width], cross_a, precision=HI) + jnp.dot(lower[:, width:], cross_b, precision=HI)
    work = work - jnp.dot(basis2, proj2, precision=MID)
    proj = jnp.concatenate([proj1, proj2], 0)
    return jnp.stack([f0, f1, f2, f3]), proj.reshape(PANELS, tile, cols), work


def solution(mesh):
    return jax.shard_map(
        on_device,
        mesh=mesh,
        in_specs=(P("row", "col"), P("row", "col"), P()),
        out_specs=(P(), P(None, None, "col"), P("row", "col")),
        check_vma=False,
    )
```

```python
import jax
import jax.numpy as jnp
from jax import lax
from jax.experimental import pallas as pl
from jax.experimental.pallas import tpu as pltpu
from jax.sharding import PartitionSpec as P

PANELS = 4
SUB = 8
HI = lax.Precision.HIGHEST
MID = lax.Precision.HIGH


def swap(x, axis, bit):
    size = lax.axis_size(axis)
    return lax.ppermute(x, axis, [(i, i ^ bit) for i in range(size)])


def bits_of(size):
    return [1 << k for k in range(size.bit_length() - 1)]


def has(axis, bit):
    return (lax.axis_index(axis) // bit) % 2


def after(x, *others):
    return lax.optimization_barrier((x, *others))[0]


def halves(x, b):
    half = x.shape[0] // 2
    return lax.dynamic_slice_in_dim(x, b * half, half, 0), lax.dynamic_slice_in_dim(x, (1 - b) * half, half, 0)


def join(mine, other, b):
    return jnp.where(b == 0, jnp.concatenate([mine, other], 0), jnp.concatenate([other, mine], 0))


def dot_t(a, b, precision=HI):
    return lax.dot_general(a, b, (((0,), (0,)), ((), ())), precision=precision)


def dot_nt(a, b, precision=HI):
    return lax.dot_general(a, b, (((1,), (1,)), ((), ())), precision=precision)


def cut_kernel(order_ref, mask_ref, matrix_ref, out_ref, *, first):
    rows, tile = out_ref.shape
    nb = mask_ref.shape[1]
    b = order_ref[first + pl.program_id(0)]
    mine = jnp.where(b // nb == lax.axis_index("col"), 1.0, 0.0)

    def step(t, carry):
        keep = mine * mask_ref[t, b % nb].astype(jnp.float32)
        s = pl.ds(pl.multiple_of(t * tile, tile), tile)
        out_ref[s, :] = matrix_ref[s, :] * keep
        return carry

    lax.fori_loop(0, rows // tile, step, 0)


def cut_panels(matrix, tile_mask, panel_order, first, count):
    rows, cols = matrix.shape
    nb = tile_mask.shape[1]
    tile = cols // nb
    return pl.pallas_call(
        lambda *refs: cut_kernel(*refs, first=first),
        grid_spec=pltpu.PrefetchScalarGridSpec(
            num_scalar_prefetch=2,
            grid=(count,),
            in_specs=[pl.BlockSpec((rows, tile), lambda p, order, mask: (0, order[first + p] % nb))],
            out_specs=pl.BlockSpec((rows, tile), lambda p, order, mask: (0, p)),
        ),
        out_shape=jax.ShapeDtypeStruct((rows, count * tile), matrix.dtype),
    )(panel_order, tile_mask, matrix)


def eliminate(m_ref, out_ref):
    size, wide = m_ref.shape
    shape = (SUB, wide)
    sub = lax.broadcasted_iota(jnp.int32, shape, 0)
    for r0 in range(0, size, SUB):
        m8 = m_ref[r0 : r0 + SUB, :]
        c = {}
        for j in range(SUB):
            col = jnp.broadcast_to(m8[:, r0 + j : r0 + j + 1], shape)
            for i in range(j, SUB):
                c[i, j] = jnp.broadcast_to(col[i : i + 1, :], shape)
        y = [jnp.broadcast_to(m8[k : k + 1, :], shape) for k in range(SUB)]
        inv, mult = {}, {}
        for k in range(SUB):
            inv[k] = 1.0 / c[k, k]
            for j in range(k + 1, SUB):
                mult[j, k] = c[j, k] * inv[k]
            for j in range(k + 1, SUB):
                for i in range(j, SUB):
                    c[i, j] = c[i, j] - mult[i, k] * c[j, k]
                y[j] = y[j] - mult[j, k] * y[k]
        v = [None] * SUB
        for j in reversed(range(SUB)):
            v[j] = inv[j] * y[j]
            for k in reversed(range(j + 1, SUB)):
                v[j] = v[j] - mult[k, j] * v[k]
        rows, pivots = y[0], c[0, 0]
        for k in range(1, SUB):
            rows = jnp.where(sub == k, y[k], rows)
            pivots = jnp.where(sub == k, c[k, k], pivots)
        out_ref[r0 : r0 + SUB, :] = rows * lax.rsqrt(pivots)
        for t0 in range(r0 + SUB, size, SUB):
            m = m_ref[t0 : t0 + SUB, :]
            left = m
            for j in range(SUB):
                m = m - jnp.broadcast_to(left[:, r0 + j : r0 + j + 1], shape) * v[j]
            m_ref[t0 : t0 + SUB, :] = m


def eliminate_tile(tile_block, m_ref, out_ref, side_ref):
    half = tile_block.shape[0] // 2
    row = lax.broadcasted_iota(jnp.int32, (half, half), 0)
    col = lax.broadcasted_iota(jnp.int32, (half, half), 1)
    unit = jnp.where(row == col, 1.0, 0.0)
    zero = jnp.zeros((half, half), tile_block.dtype)
    m_ref[...] = jnp.concatenate([tile_block[:half, :half], unit], 1)

    def step(h, carry):
        eliminate(m_ref, out_ref.at[h])

        @pl.when(h == 0)
        def _():
            across = jnp.dot(out_ref[0][:, half:], tile_block[:half, half:], precision=HI)
            side_ref[...] = jnp.concatenate([across, across], 1)
            m_ref[...] = jnp.concatenate([tile_block[half:, half:] - dot_t(across, across), unit], 1)

        return carry

    lax.fori_loop(0, 2, step, 0)
    first, second = out_ref[0], out_ref[1]
    v0, v1 = first[:, half:], second[:, half:]
    across = side_ref[:, :half]
    below = -jnp.dot(v1, dot_t(across, v0), precision=HI)
    u0, u1 = (jnp.where(col >= row, x[:, :half], 0.0) for x in (first, second))
    upper = jnp.concatenate([jnp.concatenate([u0, across], 1), jnp.concatenate([zero, u1], 1)], 0)
    inverse = jnp.concatenate([jnp.concatenate([v0, zero], 1), jnp.concatenate([below, v1], 1)], 0)
    return upper, inverse


def factor_kernel(*refs, panel, tile):
    n_in = (2, 2, 4, 5)[panel]
    n_out = (4, 2, 4, 2)[panel]
    ins, outs, (m_ref, both_ref, side_ref, *left) = refs[:n_in], refs[n_in : n_in + n_out], refs[n_in + n_out :]
    if panel % 2 == 0:
        (gram_ref,) = left
        core = lax.axis_index("col") % 2
        half = ins[0].shape[0]
        gram_ref[pl.ds(pl.multiple_of(core * half, half), half), :] = ins[0][...]
        gram_ref[pl.ds(pl.multiple_of((1 - core) * half, half), half), :] = ins[1][...]
    if panel == 0:
        rest, old = gram_ref[...], None
    elif panel == 1:
        rest, old = ins[0][...], ins[1][...]
    elif panel == 2:
        upper, lower = ins[2][...], ins[3][...]
        side = gram_ref[:, : 2 * tile]
        across = jnp.concatenate([dot_nt(upper, side[:, :tile]), dot_nt(lower, side)], 0)
        rest = gram_ref[:, 2 * tile :] - dot_t(across, across)
        old = -jnp.concatenate(
            [dot_t(across[:tile], upper) + dot_t(across[tile:], lower[:, :tile]), dot_t(across[tile:], lower[:, tile:])], 1
        )
    else:
        rest, old = ins[0][...], ins[1][...]
    outs[0][...], v = eliminate_tile(rest[:tile, :tile], m_ref, both_ref, side_ref)
    top = v if old is None else jnp.concatenate([jnp.dot(v, old[:tile], precision=HI), v], 1)
    if panel == 3:
        outs[1][...] = jnp.zeros_like(outs[1])
        for k, done in enumerate(ins[2:]):
            outs[1][k * tile : (k + 1) * tile, : (k + 1) * tile] = done[...]
        outs[1][3 * tile :, :] = top
        return
    outs[1][...] = top
    if panel == 1:
        return
    across = jnp.dot(v, rest[:tile, tile:], precision=HI)
    outs[2][...] = rest[tile:, tile:] - dot_t(across, across)
    below = -dot_t(across, top)
    if old is not None:
        below = below + jnp.concatenate([old[tile:], jnp.zeros((tile, tile), v.dtype)], 1)
    outs[3][...] = below


def factor_step(panel, tile, dtype, *operands):
    f32 = lambda *shape: jax.ShapeDtypeStruct(shape, dtype)
    wide = (panel + 1) * tile
    out = {
        0: (f32(tile, tile), f32(tile, wide), f32(tile, tile), f32(tile, wide)),
        1: (f32(tile, tile), f32(tile, wide)),
        2: (f32(tile, tile), f32(tile, wide), f32(tile, tile), f32(tile, wide)),
        3: (f32(tile, tile), f32(wide, wide)),
    }[panel]
    scratch = [pltpu.VMEM(shape, dtype) for shape in ((tile // 2, tile), (2, tile // 2, tile), (tile // 2, tile))]
    if panel % 2 == 0:
        scratch.append(pltpu.VMEM((2 * tile, (panel + 2) * tile), dtype))
    return pl.pallas_call(
        lambda *refs: factor_kernel(*refs, panel=panel, tile=tile), out_shape=out, scratch_shapes=scratch
    )(*operands)


def on_device(matrix, tile_mask, panel_order):
    rows, cols = matrix.shape
    nb_local = tile_mask.shape[1]
    tile = cols // nb_local
    dtype = matrix.dtype
    order = bits_of(lax.axis_size("row"))
    pair, *others = bits_of(lax.axis_size("col"))
    core = has("col", pair)
    shares = lax.axis_size("col")
    index = core * (shares // 2) + lax.axis_index("col") // 2

    def share_of(gram):
        part = gram.shape[0] // shares
        return lax.dynamic_slice_in_dim(gram, index * part, part, 0)

    def side_by_side(mine, other):
        return jnp.where(core == 0, jnp.concatenate([mine, other], 1), jnp.concatenate([other, mine], 1))

    mine = [cut_panels(matrix, tile_mask, panel_order, h, 2) for h in range(0, PANELS, 2)]
    work = (
        matrix.reshape(rows // tile, tile, nb_local, tile)
        * tile_mask.astype(jnp.float32)[:, None, :, None]
    ).reshape(rows, cols)
    both = [mine[h] + swap(mine[h], "col", pair) for h in range(2)]
    part = [lax.dynamic_slice_in_dim(x, core * tile, tile, 1) for x in both]
    for bit in others:
        part[0] = part[0] + swap(part[0], "col", bit)
    first = side_by_side(part[0], swap(part[0], "col", pair))

    last = len(order) - 1
    swapped = [order[1], order[0]] + order[2:]

    def halve(x, bit, *gates):
        keep, send = halves(x, has("row", bit))
        got = swap(send, "row", bit)
        return after(keep, *gates) + got

    def add(x, bit, *gates):
        got = swap(x, "row", bit)
        return after(x, *gates) + got

    def double(x, axis, bit, *gates):
        got = swap(x, axis, bit)
        return join(after(x, *gates), got, has(axis, bit))

    early = order[:last]
    crossed = swapped[:last]
    sent_a = []

    gram_a = share_of(dot_t(first, first))
    cross_a = dot_t(after(first, gram_a), work, MID)
    wait = [(cross_a,)] + [()] * last
    for k, bit in enumerate(order):
        sent_a.append(gram_a)
        gram_a = add(gram_a, bit, *wait[k])
    part[1] = after(part[1], part[0])
    for k, bit in enumerate(others):
        got = swap(part[1], "col", bit)
        part[1] = (part[1] if k else after(part[1], sent_a[last])) + got
    second = side_by_side(part[1], swap(part[1], "col", pair))
    for bit in others:
        gram_a = double(gram_a, "col", bit)
    gram_a_other = swap(gram_a, "col", pair)

    gram_b = jnp.concatenate([share_of(dot_t(second, first)), share_of(dot_t(second, second))], 1)
    cross_b = dot_t(after(second, gram_b), work, MID)
    cross_a = halve(cross_a, early[0], gram_b)
    f0, top0, rest, below = factor_step(0, tile, dtype, after(gram_a, cross_b), gram_a_other)
    gram_b = add(gram_b, order[0], f0)
    f1, top1 = factor_step(1, tile, dtype, after(rest, gram_b), below)
    for bit in early[1:]:
        cross_a = halve(cross_a, bit, f1)
    for k, bit in enumerate(order[1:]):
        gram_b = add(gram_b, bit, *((f1,) if k == 0 else ()))
        if k == 0:
            third = gram_b
    cross_b = halve(cross_b, crossed[0], third)
    for bit in crossed[1:]:
        cross_b = halve(cross_b, bit, gram_b)
    for bit in others:
        gram_b = double(gram_b, "col", bit)
    gram_b_other = swap(gram_b, "col", pair)
    f2, top2, rest, below = factor_step(2, tile, dtype, gram_b, gram_b_other, top0, top1)
    cross_a = add(cross_a, order[last], gram_b)
    cross_b = add(cross_b, order[last], f2)
    f3, inverse = factor_step(3, tile, dtype, rest, below, top0, top1, top2)
    for k, bit in enumerate(reversed(early)):
        cross_a = double(cross_a, "row", bit, f3 if k else f2)
    for bit in reversed(crossed):
        back_b = cross_b
        cross_b = double(cross_b, "row", bit, f3)
    width = 2 * tile
    basis = dot_nt(jnp.concatenate([after(first, back_b, f3), second], 1), inverse, MID)
    proj1 = jnp.dot(inverse[:width, :width], cross_a, precision=MID)
    work = lax.optimization_barrier(work - jnp.dot(basis[:, :width], proj1, precision=MID))
    proj2 = jnp.dot(inverse[width:, :width], cross_a, precision=MID) + jnp.dot(inverse[width:, width:], cross_b, precision=MID)
    work = work - jnp.dot(basis[:, width:], proj2, precision=MID)
    proj = jnp.concatenate([proj1, proj2], 0)
    return jnp.stack([f0, f1, f2, f3]), proj.reshape(PANELS, tile, cols), work


def solution(mesh):
    return jax.shard_map(
        on_device,
        mesh=mesh,
        in_specs=(P("row", "col"), P("row", "col"), P()),
        out_specs=(P(), P(None, None, "col"), P("row", "col")),
        check_vma=False,
    )
```

```python
import jax
import jax.numpy as jnp
from jax import lax
from jax.experimental import pallas as pl
from jax.experimental.pallas import tpu as pltpu
from jax.sharding import PartitionSpec as P

PANELS = 4
SUB = 8
HI = lax.Precision.HIGHEST
MID = lax.Precision.HIGH


def swap(x, axis, bit):
    size = lax.axis_size(axis)
    return lax.ppermute(x, axis, [(i, i ^ bit) for i in range(size)])


def bits_of(size):
    return [1 << k for k in range(size.bit_length() - 1)]


def has(axis, bit):
    return (lax.axis_index(axis) // bit) % 2


def after(x, *others):
    return lax.optimization_barrier((x, *others))[0]


def halves(x, b):
    half = x.shape[0] // 2
    return lax.dynamic_slice_in_dim(x, b * half, half, 0), lax.dynamic_slice_in_dim(x, (1 - b) * half, half, 0)


def join(mine, other, b):
    return jnp.where(b == 0, jnp.concatenate([mine, other], 0), jnp.concatenate([other, mine], 0))


def dot_t(a, b, precision=HI):
    return lax.dot_general(a, b, (((0,), (0,)), ((), ())), precision=precision)


def dot_nt(a, b, precision=HI):
    return lax.dot_general(a, b, (((1,), (1,)), ((), ())), precision=precision)


def cut_kernel(order_ref, mask_ref, matrix_ref, out_ref, *, first):
    rows, tile = out_ref.shape
    nb = mask_ref.shape[1]
    b = order_ref[first + pl.program_id(0)]
    mine = jnp.where(b // nb == lax.axis_index("col"), 1.0, 0.0)

    def step(t, carry):
        keep = mine * mask_ref[t, b % nb].astype(jnp.float32)
        s = pl.ds(pl.multiple_of(t * tile, tile), tile)
        out_ref[s, :] = matrix_ref[s, :] * keep
        return carry

    lax.fori_loop(0, rows // tile, step, 0)


def cut_panels(matrix, tile_mask, panel_order, first, count):
    rows, cols = matrix.shape
    nb = tile_mask.shape[1]
    tile = cols // nb
    return pl.pallas_call(
        lambda *refs: cut_kernel(*refs, first=first),
        grid_spec=pltpu.PrefetchScalarGridSpec(
            num_scalar_prefetch=2,
            grid=(count,),
            in_specs=[pl.BlockSpec((rows, tile), lambda p, order, mask: (0, order[first + p] % nb))],
            out_specs=pl.BlockSpec((rows, tile), lambda p, order, mask: (0, p)),
        ),
        out_shape=jax.ShapeDtypeStruct((rows, count * tile), matrix.dtype),
    )(panel_order, tile_mask, matrix)


def eliminate(m_ref, out_ref):
    size, wide = m_ref.shape
    shape = (SUB, wide)
    sub = lax.broadcasted_iota(jnp.int32, shape, 0)
    for r0 in range(0, size, SUB):
        m8 = m_ref[r0 : r0 + SUB, :]
        c = {}
        for j in range(SUB):
            col = jnp.broadcast_to(m8[:, r0 + j : r0 + j + 1], shape)
            for i in range(j, SUB):
                c[i, j] = jnp.broadcast_to(col[i : i + 1, :], shape)
        y = [jnp.broadcast_to(m8[k : k + 1, :], shape) for k in range(SUB)]
        inv, mult = {}, {}
        for k in range(SUB):
            inv[k] = 1.0 / c[k, k]
            for j in range(k + 1, SUB):
                mult[j, k] = c[j, k] * inv[k]
            for j in range(k + 1, SUB):
                for i in range(j, SUB):
                    c[i, j] = c[i, j] - mult[i, k] * c[j, k]
                y[j] = y[j] - mult[j, k] * y[k]
        v = [None] * SUB
        for j in reversed(range(SUB)):
            v[j] = inv[j] * y[j]
            for k in reversed(range(j + 1, SUB)):
                v[j] = v[j] - mult[k, j] * v[k]
        rows, pivots = y[0], c[0, 0]
        for k in range(1, SUB):
            rows = jnp.where(sub == k, y[k], rows)
            pivots = jnp.where(sub == k, c[k, k], pivots)
        out_ref[r0 : r0 + SUB, :] = rows * lax.rsqrt(pivots)
        for t0 in range(r0 + SUB, size, SUB):
            m = m_ref[t0 : t0 + SUB, :]
            left = m
            for j in range(SUB):
                m = m - jnp.broadcast_to(left[:, r0 + j : r0 + j + 1], shape) * v[j]
            m_ref[t0 : t0 + SUB, :] = m


def eliminate_tile(tile_block, m_ref, out_ref, side_ref):
    half = tile_block.shape[0] // 2
    row = lax.broadcasted_iota(jnp.int32, (half, half), 0)
    col = lax.broadcasted_iota(jnp.int32, (half, half), 1)
    unit = jnp.where(row == col, 1.0, 0.0)
    zero = jnp.zeros((half, half), tile_block.dtype)
    m_ref[...] = jnp.concatenate([tile_block[:half, :half], unit], 1)

    def step(h, carry):
        eliminate(m_ref, out_ref.at[h])

        @pl.when(h == 0)
        def _():
            across = jnp.dot(out_ref[0][:, half:], tile_block[:half, half:], precision=HI)
            side_ref[...] = jnp.concatenate([across, across], 1)
            m_ref[...] = jnp.concatenate([tile_block[half:, half:] - dot_t(across, across), unit], 1)

        return carry

    lax.fori_loop(0, 2, step, 0)
    first, second = out_ref[0], out_ref[1]
    v0, v1 = first[:, half:], second[:, half:]
    across = side_ref[:, :half]
    below = -jnp.dot(v1, dot_t(across, v0), precision=HI)
    u0, u1 = (jnp.where(col >= row, x[:, :half], 0.0) for x in (first, second))
    upper = jnp.concatenate([jnp.concatenate([u0, across], 1), jnp.concatenate([zero, u1], 1)], 0)
    inverse = jnp.concatenate([jnp.concatenate([v0, zero], 1), jnp.concatenate([below, v1], 1)], 0)
    return upper, inverse


def factor_kernel(*refs, panel, tile):
    n_in = (2, 2, 4, 5)[panel]
    n_out = (4, 2, 4, 2)[panel]
    ins, outs, (m_ref, both_ref, side_ref, *left) = refs[:n_in], refs[n_in : n_in + n_out], refs[n_in + n_out :]
    if panel % 2 == 0:
        (gram_ref,) = left
        core = lax.axis_index("col") % 2
        half = ins[0].shape[0]
        gram_ref[pl.ds(pl.multiple_of(core * half, half), half), :] = ins[0][...]
        gram_ref[pl.ds(pl.multiple_of((1 - core) * half, half), half), :] = ins[1][...]
    if panel == 0:
        rest, old = gram_ref[...], None
    elif panel == 1:
        rest, old = ins[0][...], ins[1][...]
    elif panel == 2:
        upper, lower = ins[2][...], ins[3][...]
        side = gram_ref[:, : 2 * tile]
        across = jnp.concatenate([dot_nt(upper, side[:, :tile]), dot_nt(lower, side)], 0)
        rest = gram_ref[:, 2 * tile :] - dot_t(across, across)
        old = -jnp.concatenate(
            [dot_t(across[:tile], upper) + dot_t(across[tile:], lower[:, :tile]), dot_t(across[tile:], lower[:, tile:])], 1
        )
    else:
        rest, old = ins[0][...], ins[1][...]
    outs[0][...], v = eliminate_tile(rest[:tile, :tile], m_ref, both_ref, side_ref)
    top = v if old is None else jnp.concatenate([jnp.dot(v, old[:tile], precision=HI), v], 1)
    if panel == 3:
        outs[1][...] = jnp.zeros_like(outs[1])
        for k, done in enumerate(ins[2:]):
            outs[1][k * tile : (k + 1) * tile, : (k + 1) * tile] = done[...]
        outs[1][3 * tile :, :] = top
        return
    outs[1][...] = top
    if panel == 1:
        return
    across = jnp.dot(v, rest[:tile, tile:], precision=HI)
    outs[2][...] = rest[tile:, tile:] - dot_t(across, across)
    below = -dot_t(across, top)
    if old is not None:
        below = below + jnp.concatenate([old[tile:], jnp.zeros((tile, tile), v.dtype)], 1)
    outs[3][...] = below


def factor_step(panel, tile, dtype, *operands):
    f32 = lambda *shape: jax.ShapeDtypeStruct(shape, dtype)
    wide = (panel + 1) * tile
    out = {
        0: (f32(tile, tile), f32(tile, wide), f32(tile, tile), f32(tile, wide)),
        1: (f32(tile, tile), f32(tile, wide)),
        2: (f32(tile, tile), f32(tile, wide), f32(tile, tile), f32(tile, wide)),
        3: (f32(tile, tile), f32(wide, wide)),
    }[panel]
    scratch = [pltpu.VMEM(shape, dtype) for shape in ((tile // 2, tile), (2, tile // 2, tile), (tile // 2, tile))]
    if panel % 2 == 0:
        scratch.append(pltpu.VMEM((2 * tile, (panel + 2) * tile), dtype))
    return pl.pallas_call(
        lambda *refs: factor_kernel(*refs, panel=panel, tile=tile), out_shape=out, scratch_shapes=scratch
    )(*operands)


def on_device(matrix, tile_mask, panel_order):
    rows, cols = matrix.shape
    nb_local = tile_mask.shape[1]
    tile = cols // nb_local
    dtype = matrix.dtype
    order = bits_of(lax.axis_size("row"))
    pair, *others = bits_of(lax.axis_size("col"))
    core = has("col", pair)
    shares = lax.axis_size("col")
    index = core * (shares // 2) + lax.axis_index("col") // 2

    def share_of(gram):
        part = gram.shape[0] // shares
        return lax.dynamic_slice_in_dim(gram, index * part, part, 0)

    def side_by_side(mine, other):
        return jnp.where(core == 0, jnp.concatenate([mine, other], 1), jnp.concatenate([other, mine], 1))

    mine = [cut_panels(matrix, tile_mask, panel_order, h, 2) for h in range(0, PANELS, 2)]
    work = (
        matrix.reshape(rows // tile, tile, nb_local, tile)
        * tile_mask.astype(jnp.float32)[:, None, :, None]
    ).reshape(rows, cols)
    both = [mine[h] + swap(mine[h], "col", pair) for h in range(2)]
    part = [lax.dynamic_slice_in_dim(x, core * tile, tile, 1) for x in both]
    for bit in others:
        part[0] = part[0] + swap(part[0], "col", bit)
    first = side_by_side(part[0], swap(part[0], "col", pair))

    last = len(order) - 1
    swapped = [order[1], order[0]] + order[2:]

    def halve(x, bit, *gates):
        keep, send = halves(x, has("row", bit))
        got = swap(send, "row", bit)
        return after(keep, *gates) + got

    def add(x, bit, *gates):
        got = swap(x, "row", bit)
        return after(x, *gates) + got

    def double(x, axis, bit, *gates):
        got = swap(x, axis, bit)
        return join(after(x, *gates), got, has(axis, bit))

    early = order[:last]
    crossed = swapped[:last]
    sent_a = []

    gram_a = share_of(dot_t(first, first))
    cross_a = dot_t(after(first, gram_a), work, MID)
    wait = [(cross_a,)] + [()] * last
    for k, bit in enumerate(order):
        sent_a.append(gram_a)
        gram_a = add(gram_a, bit, *wait[k])
    part[1] = after(part[1], part[0])
    for k, bit in enumerate(others):
        got = swap(part[1], "col", bit)
        part[1] = (part[1] if k else after(part[1], sent_a[last])) + got
    second = side_by_side(part[1], swap(part[1], "col", pair))
    for bit in others:
        gram_a = double(gram_a, "col", bit)
    gram_a_other = swap(gram_a, "col", pair)

    gram_b = jnp.concatenate([share_of(dot_t(second, first)), share_of(dot_t(second, second))], 1)
    cross_b = dot_t(after(second, gram_b), work, MID)
    cross_a = halve(cross_a, early[0], gram_b)
    f0, top0, rest, below = factor_step(0, tile, dtype, after(gram_a, cross_b), gram_a_other)
    gram_b = add(gram_b, order[0], f0)
    f1, top1 = factor_step(1, tile, dtype, after(rest, gram_b), below)
    for bit in early[1:]:
        cross_a = halve(cross_a, bit, f1)
    for k, bit in enumerate(order[1:]):
        gram_b = add(gram_b, bit, *((f1,) if k == 0 else ()))
        if k == 0:
            third = gram_b
    cross_b = halve(cross_b, crossed[0], third)
    for bit in crossed[1:]:
        cross_b = halve(cross_b, bit, gram_b)
    for bit in others:
        gram_b = double(gram_b, "col", bit)
    gram_b_other = swap(gram_b, "col", pair)
    f2, top2, rest, below = factor_step(2, tile, dtype, gram_b, gram_b_other, top0, top1)
    cross_a = add(cross_a, order[last], gram_b)
    cross_b = add(cross_b, order[last], f2)
    f3, inverse = factor_step(3, tile, dtype, rest, below, top0, top1, top2)
    for k, bit in enumerate(reversed(early)):
        cross_a = double(cross_a, "row", bit, f3 if k else f2)
    for bit in reversed(crossed):
        back_b = cross_b
        cross_b = double(cross_b, "row", bit, f3)
    width = 2 * tile
    basis1 = dot_nt(first, after(inverse[:width, :width], back_b), MID)
    basis2 = dot_nt(first, after(inverse[width:, :width], back_b), MID) + dot_nt(second, inverse[width:, width:], MID)
    factors = jnp.stack([f0, f1, f2, after(f3, back_b)])
    proj1 = jnp.dot(inverse[:width, :width], cross_a, precision=MID)
    proj = lax.optimization_barrier(jnp.pad(proj1, ((0, width), (0, 0))))
    work = lax.optimization_barrier(work - jnp.dot(basis1, proj1, precision=MID))
    proj2 = jnp.dot(inverse[width:, :width], cross_a, precision=MID) + jnp.dot(inverse[width:, width:], cross_b, precision=MID)
    work = work - jnp.dot(basis2, proj2, precision=MID)
    proj = lax.dynamic_update_slice(proj, proj2, (width, 0))
    return factors, proj.reshape(PANELS, tile, cols), work


def solution(mesh):
    return jax.shard_map(
        on_device,
        mesh=mesh,
        in_specs=(P("row", "col"), P("row", "col"), P()),
        out_specs=(P(), P(None, None, "col"), P("row", "col")),
        check_vma=False,
    )
```
